32 devices in a mesh: rows: 16 (over z, y, x), cols: 2 (over core).
Axes of the slice: x: 2, y: 2, z: 4, core: 2. Of those that a mesh axis runs over, the one named last changes fastest.
Arguments:
- slab: float32 [2048, 16384], P('rows', 'cols'), may hold values from -200 to 200, as said below
Outputs:
- r_rows: float32 [192, 16384], P(None, 'cols')
- updated: float32 [2048, 16384], P('rows', 'cols')
The draws below stay inside these ranges and needn't reach their ends.
Inputs may be any that keep to these rules, and one draw needn't show every extreme that they name: `slab`: Real-valued activations; every panel has full column rank.
All inputs are finite; a program needn't handle non-finite values.
Results may differ from the reference program's by a relative error of at most 0.0003.
Values sent between devices are 32-bit elements; how exact they have to be, the bound alone decides.
No kernel may reach another device: no remote copies, remote signals or barrier semaphores. Data moves between devices by JAX's collectives and lax.ppermute only.
A program may use at most 64 MiB of HBM per device.

```python
import math
import jax
import jax.numpy as jnp
from jax import lax

D = 16384
PANEL = 64
PANELS = 3
TOKENS = 2048
N_COLS = 2


def draw_slab(key, part):
    key_one, key_two, key_three = jax.random.split(jax.random.fold_in(key, 7), 3)
    position = jnp.arange(TOKENS, dtype=jnp.float32) / TOKENS
    noise = jnp.clip(jax.random.normal(key_one, (TOKENS, D), jnp.float32), -4.0, 4.0)
    growth = 3.0 ** position
    rowscale = jnp.exp(jax.random.uniform(key_two, (TOKENS, 1), jnp.float32, math.log(0.3), math.log(3.0)))
    colscale = jnp.exp(jax.random.uniform(key_three, (1, D), jnp.float32, math.log(0.3), math.log(3.0)))
    return noise * rowscale * growth[:, None] * colscale


def setup_inputs(seed: int = 0) -> dict:
    key_list = jax.random.split(jax.random.key(seed), 2)
    slab = draw_slab(jax.random.fold_in(key_list[1], 71), 0)
    return {"slab": slab}


def reference(slab):
    current = slab
    col_count = D // N_COLS
    blocks = []
    for turn in range(PANELS):
        first_col = turn % N_COLS * col_count + turn // N_COLS * PANEL
        panel_cols = current[:, first_col:first_col + PANEL]
        basis, upper = jnp.linalg.qr(panel_cols)
        basis = basis * jnp.sign(jnp.diagonal(upper))[None, :]
        coeffs = jnp.dot(basis.T, current, precision=lax.Precision.HIGHEST)
        current = current - jnp.dot(basis, coeffs, precision=lax.Precision.HIGHEST)
        blocks.append(coeffs / jnp.sqrt(jnp.float32(TOKENS)))
    return (jnp.concatenate(blocks, 0), current)
```

```python
import functools
import math

import jax
import jax.numpy as jnp
from jax import lax
from jax.experimental import pallas as pl
from jax.experimental.pallas import tpu as pltpu
from jax.sharding import PartitionSpec as P

PANEL = 64
PANELS = 3
BASIS = PANEL * PANELS
SUBLANES = 8
CHUNKS = 4

dot = functools.partial(
    jnp.dot, precision=lax.Precision.HIGHEST, preferred_element_type=jnp.float32
)


def swap(value, bit):
    size = lax.axis_size("rows")
    return lax.ppermute(value, "rows", [(i, i ^ (1 << bit)) for i in range(size)])


def gather_panels(front):
    col_total = lax.axis_size("cols")
    here = lax.axis_index("cols")
    fronts = [front]
    for shift in range(1, col_total):
        pairs = [(i, (i + shift) % col_total) for i in range(col_total)]
        fronts.append(lax.ppermute(front, "cols", pairs))
    panels = []
    for turn in range(PANELS):
        away = lax.rem(here - turn % col_total + col_total, col_total)
        offset = turn // col_total * PANEL
        panel = fronts[0][:, offset : offset + PANEL]
        for shift in range(1, col_total):
            other = fronts[shift][:, offset : offset + PANEL]
            panel = jnp.where(away == shift, other, panel)
        panels.append(panel)
    return jnp.concatenate(panels, 1)


def orders(row_bits, chunk):
    rest = list(range(2, row_bits))
    if chunk == CHUNKS - 1 or row_bits < 3:
        return [0, 1] + rest, [1, 0] + rest
    return [0, 2, 1] + rest[1:], [1, 2, 0] + rest[1:]


class Stream:
    def __init__(self, slab, me, start, width, order):
        self.me, self.start, self.half, self.order = me, start, width // 2, order
        self.raw = self.bit(order[0])
        self.split = 0
        while self.split < len(order) - 1 and (BASIS >> (self.split + 1)) % SUBLANES == 0:
            self.split += 1
        mine = lax.dynamic_slice_in_dim(slab, start + self.raw * self.half, self.half, 1)
        theirs = lax.dynamic_slice_in_dim(slab, start + (1 - self.raw) * self.half, self.half, 1)
        self.mine = mine
        self.got = swap(theirs, order[0])

    def bit(self, place):
        return lax.rem(lax.div(self.me, 1 << place), 2)

    def reduce(self, panels_t, partner_panels_t):
        rows = BASIS // 2
        def part(which):
            own = lax.dynamic_slice_in_dim(panels_t, which * rows, rows, 0)
            other = lax.dynamic_slice_in_dim(partner_panels_t, which * rows, rows, 0)
            return dot(own, self.mine) + dot(other, self.got)
        side = self.bit(self.order[1])
        sent = part(1 - side)
        block = part(side) + swap(sent, self.order[1])
        for place in self.order[2 : 1 + self.split]:
            rows //= 2
            side = self.bit(place)
            sent = lax.dynamic_slice_in_dim(block, (1 - side) * rows, rows, 0)
            kept = lax.dynamic_slice_in_dim(block, side * rows, rows, 0)
            block = kept + swap(sent, place)
        for place in self.order[1 + self.split :]:
            block = block + swap(block, place)
        self.block = block

    def spread(self):
        block = self.block
        for place in reversed(self.order[1 : 1 + self.split]):
            block = jnp.concatenate([block, swap(block, place)], 0)
        self.kept, self.other = block, swap(block, self.order[0])

    def place(self):
        index = self.me * 0
        for place in self.order[1 : 1 + self.split]:
            index = index * 2 + self.bit(place)
        return index

    def leading(self, count):
        first = jnp.where(self.raw == 0, self.kept[:, :count], self.other[:, :count])
        pieces = 1 << self.split
        rows = BASIS // pieces
        index = self.place()
        return jnp.concatenate(
            [
                lax.dynamic_slice_in_dim(first, lax.bitwise_xor(index, q) * rows, rows, 0)
                for q in range(pieces)
            ],
            0,
        )


def finish_kernel(pieces, scale, where, kept, other, slab, inverse, basis, *refs):
    r_out, up_out, whole = refs[-3:]
    rows = BASIS // pieces
    index = where[0]

    def fill(source):
        for p in range(pieces):
            at = pl.multiple_of((index ^ p) * rows, SUBLANES)
            whole[pl.ds(at, rows), :] = source[p * rows : (p + 1) * rows, :]

    pl.when(pl.program_id(0) == 0)(lambda: fill(kept))
    pl.when(pl.program_id(0) == 1)(lambda: fill(other))
    coeffs = dot(inverse[...], whole[...])
    r_out[...] = coeffs * scale
    up_out[...] = slab[...] - dot(basis[...], coeffs)


def finish(stream, slab, inverse, basis, scale, earlier):
    pieces = 1 << stream.split
    half = stream.half
    rows_here, width = slab.shape
    where = jnp.stack([stream.place(), stream.raw]).astype(jnp.int32)
    base = stream.start // half

    def column(side, where):
        return (0, base + (where[1] ^ side))

    def whole(side, where):
        return (0, 0)

    any_space = pl.BlockSpec(memory_space=pl.ANY)
    return pl.pallas_call(
        functools.partial(finish_kernel, pieces, scale),
        out_shape=(
            jax.ShapeDtypeStruct((BASIS, width), jnp.float32),
            jax.ShapeDtypeStruct((rows_here, width), jnp.float32),
        ),
        grid_spec=pltpu.PrefetchScalarGridSpec(
            num_scalar_prefetch=1,
            grid=(2,),
            in_specs=[
                pl.BlockSpec((BASIS, half), whole),
                pl.BlockSpec((BASIS, half), whole),
                pl.BlockSpec((rows_here, half), column),
                pl.BlockSpec((BASIS, BASIS), whole),
                pl.BlockSpec((rows_here, BASIS), whole),
            ]
            + [any_space] * len(earlier),
            out_specs=(
                pl.BlockSpec((BASIS, half), column),
                pl.BlockSpec((rows_here, half), column),
            ),
            scratch_shapes=[pltpu.VMEM((BASIS, half), jnp.float32)],
        ),
        input_output_aliases={6: 0, 7: 1} if earlier else {},
        name="finish",
    )(where, stream.kept, stream.other, slab, inverse, basis, *earlier)


def on_device(slab):
    rows_here, width = slab.shape
    row_total = lax.axis_size("rows")
    row_bits = row_total.bit_length() - 1
    assert row_total == 1 << row_bits and row_bits >= 2
    scale = 1.0 / math.sqrt(rows_here * row_total)
    me = lax.axis_index("rows")
    lead = -(-PANELS // lax.axis_size("cols")) * PANEL

    panels = gather_panels(slab[:, :lead])
    panels_t = panels.T
    partner_t = [swap(panels_t, 0), swap(panels_t, 1)]
    wide = width // (2 * CHUNKS)
    streams = []
    for chunk in range(CHUNKS):
        for color, order in enumerate(orders(row_bits, chunk)):
            start = (2 * chunk + color) * wide
            streams.append(Stream(slab, me, start, wide, order))
    for stream in streams:
        stream.reduce(panels_t, partner_t[stream.order[0]])
    for stream in streams:
        stream.spread()
    gram = gather_panels(streams[0].leading(lead))
    factor = jnp.linalg.cholesky(gram, symmetrize_input=False)
    inverse = jax.scipy.linalg.solve_triangular(
        factor, jnp.eye(BASIS, dtype=jnp.float32), lower=True
    )
    basis = dot(panels, inverse.T)
    done = ()
    for stream in streams:
        done = finish(stream, slab, inverse, basis, scale, done)
    return tuple(done)


def solution(mesh):
    placed = (P("rows", "cols"),)
    return jax.shard_map(
        on_device,
        mesh=mesh,
        in_specs=placed,
        out_specs=(P(None, "cols"), P("rows", "cols")),
        check_vma=False,
    )
```
